512 devices in a mesh: dp: 128 (over y, z, core), grp: 4 (over x).
Axes of the slice: x: 4, y: 8, z: 8, core: 2. Of those that a mesh axis runs over, the one named last changes fastest.
Arguments:
- states: bfloat16 [65536, 2048], P(('dp', 'grp')), may hold values from -60 to 60
- projection: bfloat16 [2048, 768], replicated, may hold values from -0.125 to 0.125
- owner_group: int32 [65536, 1], P(('dp', 'grp')), may hold values from 0 to 127; in each aligned block of 128 rows (0 to 127, 128 to 255, ...) at most 2 rows name the same one
- cluster_sub: int32 [65536], P(('dp', 'grp')), may hold values from 0 to 3
- priority: int32 [65536], P(('dp', 'grp')), may hold values from 0 to 65535, each once
Outputs:
- dup_score: float32 [65536], P(('dp', 'grp'))
The draws below stay inside these ranges and needn't reach their ends.
Inputs may be any that keep to these rules, and one draw needn't show every extreme that they name: `owner_group`: in each aligned block of 128 rows (the rows of one device) no owner is named by more than 2 rows; in some block some owner is named by exactly 2 rows.
All inputs are finite; a program needn't handle non-finite values.
Results may differ from the reference program's by a relative error of at most 0.0012.
Values may be sent and summed in bfloat16 or wider, within the bound.
A program may use at most 64 MiB of HBM per device.

```python
import math
import jax
import jax.numpy as jnp
import numpy as np
from jax import lax

DIN = 2048
DE = 768
ROW_DEV = 128
SUBS = 4
SLOT = 2
ROWS = 65536
N_DP = 128


def draw_states(key, part):
    key_noise = jax.random.fold_in(key, 11)
    key_scale = jax.random.fold_in(key, 12)
    row_scale = 10.0 ** jax.random.uniform(key_scale, (ROWS, 1), jnp.float32)
    noise_draw = jax.random.normal(key_noise, (ROWS, DIN), jnp.float32)
    return (row_scale * jnp.clip(noise_draw, -6.0, 6.0)).astype(jnp.bfloat16)


def place_ends(array, own_key, low, high):
    shape = array.shape
    place = [jax.random.randint(jax.random.fold_in(own_key, axis), (), 0, shape[axis]) for axis in range(len(shape))]
    array = array.at[tuple(place)].set(low)
    longest = shape.index(max(shape))
    place[longest] = (place[longest] + 1) % shape[longest]
    return array.at[tuple(place)].set(high)


def assign_block(rng, own, number, rows, count, top, most, lean):
    order = jax.random.permutation(rng, count)
    crowded, usual = portions_of(count, rows * top, most, lean, True), portions_of(count, rows * top, most, lean, False)
    places = jnp.arange(count)

    def named(lengths, offset_by):
        used = int((lengths > 0).sum())
        fixed = max(1, used // 4)
        passed = fixed + (places - fixed + offset_by * (used - fixed)) % max(1, count - fixed)
        return jnp.zeros((count,), jnp.int32).at[order[jnp.where(places < fixed, places, passed)]].set(jnp.asarray(lengths, jnp.int32))

    lengths = jnp.where(number % 4 == 0, named(crowded, number // 4), named(usual, number - number // 4 - 1))
    mixed = jax.random.permutation(jax.random.fold_in(own, 3), count)
    giver, receiver = mixed[0:count // 2 * 2:2], mixed[1:count // 2 * 2:2]
    room = jnp.minimum(lengths[giver] - 1, most - lengths[receiver]) // 2
    room = jnp.where((giver == order[0]) | (receiver == order[0]) | (lengths[receiver] == 0), 0, jnp.maximum(room, 0))
    passed = jax.random.randint(jax.random.fold_in(own, 4), (count // 2,), 0, 1 << 20) % (room + 1)
    lengths = lengths.at[giver].add(-passed).at[receiver].add(passed)
    labels = jnp.searchsorted(jnp.cumsum(lengths), jnp.arange(rows * top), side="right").astype(jnp.int32)
    table = labels.reshape(top, rows).T
    table = table[jax.random.permutation(jax.random.fold_in(own, 1), rows)]
    offset_by = jax.random.randint(jax.random.fold_in(own, 2), (rows, 1), 0, top)
    return jnp.take_along_axis(table, (jnp.arange(top)[None, :] + offset_by) % top, axis=1)


def portions_of(amount, total, bound, slope, full):
    loads = [(1 << 20) // math.isqrt(rank ** slope) + 1 for rank in range(1, amount + 1)]
    largest = bound if full else min(bound, max(-(-total // amount), total * loads[0] // sum(loads)))
    least = 1 if total - largest >= amount - 1 else 0
    counts, surplus = [largest] + [least] * (amount - 1), total - largest - least * (amount - 1)
    while surplus > 0:
        free = [i for i in range(1, amount) if counts[i] < largest] or [i for i in range(1, amount) if counts[i] < bound]
        mass, budget = sum([loads[i] for i in free]), surplus
        for i in free:
            addition = min(bound - counts[i], max(1, budget * loads[i] // mass), surplus)
            counts[i] = counts[i] + addition
            surplus = surplus - addition
    return np.array(counts)


def gaussian(rng, shape, width, reach, held_as=jnp.bfloat16):
    return jnp.clip(width * jax.random.normal(rng, shape, jnp.float32), -reach, reach).astype(held_as)


def setup_inputs(seed: int = 0) -> dict:
    seeds = jax.random.split(jax.random.key(seed), 6)
    states = draw_states(jax.random.fold_in(seeds[5], 71), 0)
    projection = gaussian(seeds[1], (DIN, DE), DIN ** -0.5, 0.125)
    owner_group_keys = jax.random.split(jax.random.fold_in(seeds[2], 1), ROWS // ROW_DEV)
    owner_group_turns = jax.random.permutation(jax.random.fold_in(seeds[2], 3), ROWS // ROW_DEV)
    owner_group = jax.vmap(lambda own, number: assign_block(jax.random.fold_in(seeds[2], 2), own, number, ROW_DEV, N_DP, 1, SLOT, 1))(owner_group_keys, owner_group_turns).reshape((ROWS, 1))
    cluster_sub = place_ends(jax.random.randint(seeds[3], (ROWS,), 0, SUBS), jax.random.fold_in(seeds[3], 1), 0, SUBS - 1).astype(jnp.int32)
    priority = jax.random.permutation(seeds[4], ROWS).astype(jnp.int32)
    return dict(states=states, projection=projection, owner_group=owner_group, cluster_sub=cluster_sub, priority=priority)


block_rows = 256

def reference(states, projection, owner_group, cluster_sub, priority):
    projected = jnp.dot(states, projection, preferred_element_type=jnp.float32)
    square_sum = lax.optimization_barrier(jnp.sum(projected * projected, axis=1, keepdims=True))
    inverse_norm = lax.rsqrt(square_sum + 1e-06)
    embedding = (projected * inverse_norm).astype(jnp.bfloat16)
    cluster = (owner_group[:, 0] * SUBS + cluster_sub).astype(jnp.int32)
    sort_key = cluster * ROWS + priority
    sort_order = jnp.argsort(sort_key).astype(jnp.int32)
    sorted_emb = embedding[sort_order]
    sorted_cluster = cluster[sort_order]
    cluster_first = jnp.searchsorted(sorted_cluster, sorted_cluster, side='left').astype(jnp.int32)
    position = jnp.arange(ROWS, dtype=jnp.int32)

    def one_block(block_index):
        first_row = (block_index * block_rows).astype(jnp.int32)
        query_emb = lax.dynamic_slice_in_dim(sorted_emb, first_row, block_rows, 0)
        query_cl = lax.dynamic_slice_in_dim(sorted_cluster, first_row, block_rows, 0)
        query_pos = lax.dynamic_slice_in_dim(position, first_row, block_rows, 0)
        low_block = (lax.dynamic_index_in_dim(cluster_first, first_row, 0, keepdims=False) // block_rows).astype(jnp.int32)

        def key_step(key_block, running):
            key_start = (key_block * block_rows).astype(jnp.int32)
            key_emb = lax.dynamic_slice_in_dim(sorted_emb, key_start, block_rows, 0)
            key_cl = lax.dynamic_slice_in_dim(sorted_cluster, key_start, block_rows, 0)
            key_pos = lax.dynamic_slice_in_dim(position, key_start, block_rows, 0)
            cosine = jnp.dot(query_emb, key_emb.T, preferred_element_type=jnp.float32)
            earlier = (key_cl[None, :] == query_cl[:, None]) & (key_pos[None, :] < query_pos[:, None])
            return jnp.maximum(running, lax.optimization_barrier(jnp.max(jnp.where(earlier, cosine, -1.0), axis=1)))
        start_value = jnp.full((block_rows,), -1.0, jnp.float32)
        return lax.fori_loop(low_block, (block_index + 1).astype(jnp.int32), key_step, start_value)
    scores = lax.map(one_block, jnp.arange(ROWS // block_rows, dtype=jnp.int32)).reshape(ROWS)
    return jnp.zeros((ROWS,), scores.dtype).at[sort_order].set(scores)
```

```python
import functools

import jax
import jax.numpy as jnp
from jax import lax
from jax.experimental import pallas as pl
from jax.experimental.pallas import tpu as pltpu
from jax.sharding import PartitionSpec as P

MESH = pl.DeviceIdType.MESH
NY = 8
NZ = 16
NG = 4
SLOTS = 2
NT = (((1,), (1,)), ((), ()))


def mm(a, b):
    return jnp.dot(a, b, preferred_element_type=jnp.float32)


def mm_nt(a, b):
    return lax.dot_general(a, b, NT, preferred_element_type=jnp.float32)


def iota(shape, axis):
    return lax.broadcasted_iota(jnp.int32, shape, axis)


def ones_where(cond):
    return jnp.where(cond, 1.0, 0.0).astype(jnp.bfloat16)


def kernel(
    st, pr, ow, su, pi, out,
    s1a, s1b, r1a, r1b, s2a, s2b, r2a, r2b,
    krow, xa, xb, xk, sc, sr, rb, tb, rr,
    y1s, y1r, z1s, z1r, z2s, z2r, y2s, y2r, xs, xr, b1s, b1r, b2s, b2r,
):
    docs = st.shape[0]
    width = pr.shape[1]
    half = width // 2
    rows = NY * NZ * SLOTS
    ygrp = NZ * SLOTS
    zgrp = NY * SLOTS
    dp = lax.axis_index("dp")
    grp = lax.axis_index("grp")
    my_y = dp // NZ
    my_z = dp % NZ

    def y_at(i):
        return (my_y + i) % NY

    def z_at(j):
        return (my_z + j) % NZ

    def g_at(i):
        return (grp + i) % NG

    def y_dev(i):
        return {"dp": y_at(i) * NZ + my_z}

    def z_dev(j):
        return {"dp": my_y * NZ + z_at(j)}

    def g_dev(i):
        return {"grp": g_at(i)}

    def copy(src, dst, ssem, rsem, i, dev):
        return pltpu.make_async_remote_copy(
            src_ref=src, dst_ref=dst, send_sem=ssem.at[i], recv_sem=rsem.at[i],
            device_id=dev, device_id_type=MESH,
        )

    def yrows(y):
        return pl.ds(pl.multiple_of(y * ygrp, ygrp), ygrp)

    def zrows(z):
        return pl.ds(pl.multiple_of(z * zgrp, zgrp), zgrp)

    barrier = pltpu.get_barrier_semaphore()
    for i in range(1, NY):
        pl.semaphore_signal(barrier, inc=1, device_id=y_dev(i), device_id_type=MESH)
    for j in range(1, NZ):
        pl.semaphore_signal(barrier, inc=1, device_id=z_dev(j), device_id_type=MESH)
    for i in range(1, NG):
        pl.semaphore_signal(barrier, inc=1, device_id=g_dev(i), device_id_type=MESH)

    projected = mm(st[...], pr[...])
    square_sum = jnp.sum(projected * projected, axis=1, keepdims=True)
    emb = (projected * lax.rsqrt(square_sum + 1e-06)).astype(jnp.bfloat16)

    owner = ow[...]
    onehot = iota((NY * NZ, docs), 0) == owner
    before = ones_where(iota((docs, docs), 0) < iota((docs, docs), 1))
    counts = mm(ones_where(onehot), before)
    place = jnp.sum(jnp.where(onehot, counts, 0.0), axis=0, keepdims=True).astype(jnp.int32)
    target = owner * SLOTS + place
    target_b = (owner % NZ) * zgrp + (owner // NZ) * SLOTS + place
    slot_row = iota((rows, docs), 0)
    pick_a = ones_where(slot_row == target)
    pick_b = ones_where(slot_row == target_b)
    prio = pi[...]
    line = iota((docs, docs), 0)
    meta = jnp.where(
        line == 0, su[...] + 1, jnp.where(line == 1, prio // 256, jnp.where(line == 2, prio % 256, 0))
    ).astype(jnp.float32).astype(jnp.bfloat16)
    s1a[:, :half] = mm(pick_a, emb[:, :half]).astype(jnp.bfloat16)
    s1a[:, half:] = mm_nt(pick_a, meta).astype(jnp.bfloat16)
    s1b[...] = mm(pick_b, emb[:, half:]).astype(jnp.bfloat16)

    r_i, c_i = iota((rows, rows), 0), iota((rows, rows), 1)
    to_z = ones_where(c_i == ((r_i // SLOTS) % NY) * ygrp + (r_i // zgrp) * SLOTS + r_i % SLOTS)
    to_y = ones_where(c_i == ((r_i // SLOTS) % NZ) * zgrp + (r_i // ygrp) * SLOTS + r_i % SLOTS)

    pl.semaphore_wait(barrier, NY + NZ + NG - 3)
    sent = []
    y1, z1 = [], []
    for i in range(1, NY):
        c = copy(s1a.at[yrows(y_at(i)), :], r1a.at[yrows(my_y), :], y1s, y1r, i, y_dev(i))
        c.start()
        y1.append(c)
    for j in range(1, NZ):
        c = copy(s1b.at[zrows(z_at(j)), :], r1b.at[zrows(my_z), :], z1s, z1r, j, z_dev(j))
        c.start()
        z1.append(c)
    r1a[yrows(my_y), :] = s1a[yrows(my_y), :]
    r1b[zrows(my_z), :] = s1b[zrows(my_z), :]
    for c in y1:
        c.wait_recv()
    s2a[...] = mm(to_z, r1a[...]).astype(jnp.bfloat16)
    z2, y2 = [], []
    for j in range(1, NZ):
        c = copy(s2a.at[zrows(z_at(j)), :], r2a.at[zrows(my_z), :], z2s, z2r, j, z_dev(j))
        c.start()
        z2.append(c)
    r2a[zrows(my_z), :] = s2a[zrows(my_z), :]
    for c in z1:
        c.wait_recv()
    s2b[...] = mm(to_y, r1b[...]).astype(jnp.bfloat16)
    for i in range(1, NY):
        c = copy(s2b.at[yrows(y_at(i)), :], r2b.at[yrows(my_y), :], y2s, y2r, i, y_dev(i))
        c.start()
        y2.append(c)
    r2b[yrows(my_y), :] = s2b[yrows(my_y), :]

    for c in z2:
        c.wait_recv()
    qa = r2a[:, :half]
    qmeta = r2a[:, half:]
    w_row = iota((128, 128), 0)
    w_col = iota((128, 128), 1)

    def weights(at):
        return jnp.where(
            at == 0, 65536.0, jnp.where(at == 1, 256.0, jnp.where(at == 2, 1.0, 0.0))
        ).astype(jnp.bfloat16)

    krow[...] = mm_nt(weights(w_col)[:16], qmeta)[:8] - 65536.0
    ax1 = copy(r2a.at[:, pl.ds(0, half)], xa.at[0], xs, xr, 0, g_dev(1))
    ax2 = copy(r2a.at[:, pl.ds(0, half)], xa.at[1], xs, xr, 1, g_dev(NG - 1))
    ax1.start()
    ax2.start()
    kx = []
    for i in range(1, NG):
        c = copy(krow, xk.at[i - 1], xs, xr, 5 + i, g_dev(i))
        c.start()
        kx.append(c)
    for c in y2:
        c.wait_recv()
    bx2 = copy(r2b, xb.at[1], xs, xr, 3, g_dev(NG - 1))
    bx1 = copy(r2b, xb.at[0], xs, xr, 2, g_dev(1))
    bx2.start()
    bx1.start()

    qval = mm(qmeta, weights(w_row)) - 65536.0
    qbase = mm(qmeta, jnp.where(w_row == 0, 65536.0, 0.0).astype(jnp.bfloat16)) - 65536.0
    qb = mm(to_z, r2b[...]).astype(jnp.bfloat16)

    def fold(acc, ka, kb, keys):
        cosine = mm_nt(qa, ka) + mm_nt(qb, kb)
        for lane in range(0, rows, 128):
            key = keys[0:1, lane : lane + 128]
            ok = (key >= qbase) & (key < qval)
            acc = jnp.maximum(acc, jnp.where(ok, cosine[:, lane : lane + 128], -1.0))
        return acc

    acc = fold(jnp.full((rows, 128), -1.0, jnp.float32), qa, qb, krow[...])
    ax1.wait_recv()
    af = copy(xa.at[0], xa.at[2], xs, xr, 4, g_dev(1))
    af.start()
    bx2.wait_recv()
    bf = copy(xb.at[1], xb.at[2], xs, xr, 5, g_dev(NG - 1))
    bf.start()
    for c in kx:
        c.wait_recv()
    bx1.wait_recv()
    acc = fold(acc, xa[0], mm(to_z, xb[0]).astype(jnp.bfloat16), xk[0])
    ax2.wait_recv()
    acc = fold(acc, xa[1], mm(to_z, xb[1]).astype(jnp.bfloat16), xk[2])
    af.wait_recv()
    bf.wait_recv()
    acc = fold(acc, xa[2], mm(to_z, xb[2]).astype(jnp.bfloat16), xk[1])

    best = jnp.max(jnp.transpose(acc), axis=0, keepdims=True)
    per = 128 // zgrp
    for h in range(rows // 128):
        sc[h] = best[:, h * 128 : (h + 1) * 128]
    b1, b2 = [], []
    for j in range(1, NZ):
        c = copy(sc.at[z_at(j) // per], sr.at[my_z], b1s, b1r, j, z_dev(j))
        c.start()
        b1.append(c)
    sr[my_z] = sc[my_z // per]
    rb[...] = jnp.zeros_like(rb)
    for c in b1:
        c.wait_recv()
    for z in range(NZ):
        rb[z : z + 1, :] = sr[z]
    tb[...] = jnp.transpose(rb[...])

    def back_rows(y):
        return pl.ds(pl.multiple_of((my_z % per) * zgrp + (y // 4) * 8, 8), 8)

    for i in range(1, NY):
        c = copy(tb.at[back_rows(y_at(i)), :], rr.at[my_y], b2s, b2r, i, y_dev(i))
        c.start()
        b2.append(c)
    rr[my_y] = tb[back_rows(my_y), :]
    target_col = jnp.transpose(jnp.broadcast_to(target.astype(jnp.float32), (docs, docs)))
    lanes = iota((docs, 128), 1)
    res = jnp.full((docs, 128), -2.0, jnp.float32)
    for c in b2:
        c.wait_recv()
    for y in range(NY):
        for s in range(SLOTS):
            score = rr[y, pl.ds((my_y % 4) * SLOTS + s, 1), :]
            code = jnp.where(lanes < NZ, (y * NZ + lanes) * SLOTS + s, -1).astype(jnp.float32)
            res = jnp.where(target_col == code, score, res)
    out[...] = jnp.max(jnp.transpose(res), axis=0, keepdims=True)

    sent = y1 + z1 + z2 + y2 + [ax1, ax2, bx1, bx2, af, bf] + kx + b1 + b2
    for c in sent:
        c.wait_send()


def on_device(states, projection, owner_group, cluster_sub, priority):
    docs = states.shape[0]
    width = projection.shape[1]
    half = width // 2
    rows = NY * NZ * SLOTS
    bf, f32 = jnp.bfloat16, jnp.float32
    vmem = pl.BlockSpec(memory_space=pltpu.VMEM)
    dma = pltpu.SemaphoreType.DMA
    score = pl.pallas_call(
        kernel,
        out_shape=jax.ShapeDtypeStruct((1, docs), f32),
        in_specs=[vmem] * 5,
        out_specs=vmem,
        scratch_shapes=[
            pltpu.VMEM((rows, half + 128), bf),
            pltpu.VMEM((rows, half), bf),
            pltpu.VMEM((rows, half + 128), bf),
            pltpu.VMEM((rows, half), bf),
            pltpu.VMEM((rows, half + 128), bf),
            pltpu.VMEM((rows, half), bf),
            pltpu.VMEM((rows, half + 128), bf),
            pltpu.VMEM((rows, half), bf),
            pltpu.VMEM((8, rows), f32),
            pltpu.VMEM((3, rows, half), bf),
            pltpu.VMEM((3, rows, half), bf),
            pltpu.VMEM((3, 8, rows), f32),
            pltpu.VMEM((rows // 128, 1, 128), f32),
            pltpu.VMEM((NZ, 1, 128), f32),
            pltpu.VMEM((128, 128), f32),
            pltpu.VMEM((128, 128), f32),
            pltpu.VMEM((NY, 8, 128), f32),
            dma((NY,)), dma((NY,)), dma((NZ,)), dma((NZ,)),
            dma((NZ,)), dma((NZ,)), dma((NY,)), dma((NY,)),
            dma((9,)), dma((9,)),
            dma((NZ,)), dma((NZ,)), dma((NY,)), dma((NY,)),
        ],
        compiler_params=pltpu.CompilerParams(
            collective_id=0, has_side_effects=True, vmem_limit_bytes=48 * 1024 * 1024
        ),
    )(
        states,
        projection,
        owner_group.reshape(1, docs),
        cluster_sub.reshape(1, docs),
        priority.reshape(1, docs),
    )
    return score.reshape(docs)


def solution(mesh):
    in_specs = (
        P(("dp", "grp"), None),
        P(),
        P(("dp", "grp"), None),
        P(("dp", "grp")),
        P(("dp", "grp")),
    )
    return jax.shard_map(
        on_device, mesh=mesh, in_specs=in_specs, out_specs=P(("dp", "grp")), check_vma=False
    )
```

```python
import functools

import jax
import jax.numpy as jnp
from jax import lax
from jax.experimental import pallas as pl
from jax.experimental.pallas import tpu as pltpu
from jax.sharding import PartitionSpec as P

MESH = pl.DeviceIdType.MESH
NY = 8
NZ = 16
NG = 4
SLOTS = 2
LOADS = 4
PARTS = 2
FIRST = 1
NT = (((1,), (1,)), ((), ()))
Y_FAR = sorted(range(1, NY), key=lambda i: -min(i, NY - i))
Z_FAR = sorted(range(1, NZ), key=lambda j: -min(j, NZ - j))


def mm(a, b):
    return jnp.dot(a, b, preferred_element_type=jnp.float32)


def mm_nt(a, b):
    return lax.dot_general(a, b, NT, preferred_element_type=jnp.float32)


def iota(shape, axis):
    return lax.broadcasted_iota(jnp.int32, shape, axis)


def ones_where(cond):
    return jnp.where(cond, 1.0, 0.0).astype(jnp.bfloat16)


def kernel(
    st_hbm, pr_hbm, ow_hbm, su_hbm, pi_hbm, out,
    st, pr, ow, su, pi, load,
    s1a, s1b, r1a, r1b, s2a, s2b, r2a, r2b,
    krow, xa, xb, xk, sc, sr, rb, tb, rr,
    y1s, y1r, z1s, z1r, z2s, z2r, y2s, y2r, xs, xr, b1s, b1r, b2s, b2r,
):
    docs = st.shape[0]
    depth, width = pr.shape
    half = width // 2
    meta_w = s1a.shape[1] - half
    parts = PARTS
    first = FIRST * 128
    x_cols = [(0, first), (first, half - first)]
    a_cols = [(0, meta_w + first), (meta_w + first, half - first)]
    step = depth // LOADS
    rows = NY * NZ * SLOTS
    ygrp = NZ * SLOTS
    zgrp = NY * SLOTS
    dp = lax.axis_index("dp")
    grp = lax.axis_index("grp")
    my_y = dp // NZ
    my_z = dp % NZ

    def y_at(i):
        return (my_y + i) % NY

    def z_at(j):
        return (my_z + j) % NZ

    def g_at(i):
        return (grp + i) % NG

    def y_dev(i):
        return {"dp": y_at(i) * NZ + my_z}

    def z_dev(j):
        return {"dp": my_y * NZ + z_at(j)}

    def g_dev(i):
        return {"grp": g_at(i)}

    def copy(src, dst, ssem, rsem, i, dev):
        return pltpu.make_async_remote_copy(
            src_ref=src, dst_ref=dst, send_sem=ssem.at[i], recv_sem=rsem.at[i],
            device_id=dev, device_id_type=MESH,
        )

    def yrows(y):
        return pl.ds(pl.multiple_of(y * ygrp, ygrp), ygrp)

    def zrows(z):
        return pl.ds(pl.multiple_of(z * zgrp, zgrp), zgrp)

    barrier = pltpu.get_barrier_semaphore()
    for i in range(1, NY):
        pl.semaphore_signal(barrier, inc=1, device_id=y_dev(i), device_id_type=MESH)
    for j in range(1, NZ):
        pl.semaphore_signal(barrier, inc=1, device_id=z_dev(j), device_id_type=MESH)
    for i in range(1, NG):
        pl.semaphore_signal(barrier, inc=1, device_id=g_dev(i), device_id_type=MESH)

    loads = []
    for i, (src, dst) in enumerate(((ow_hbm, ow), (su_hbm, su), (pi_hbm, pi))):
        loads.append(pltpu.make_async_copy(src, dst, load.at[i]))
    for i in range(LOADS):
        cut = pl.ds(i * step, step)
        loads.append(pltpu.make_async_copy(st_hbm.at[:, cut], st.at[:, cut], load.at[3 + 2 * i]))
        loads.append(pltpu.make_async_copy(pr_hbm.at[cut, :], pr.at[cut, :], load.at[4 + 2 * i]))
    for c in loads:
        c.start()
    for c in loads[:3]:
        c.wait()
    owner = ow[...]
    onehot = iota((NY * NZ, docs), 0) == owner
    before = ones_where(iota((docs, docs), 0) < iota((docs, docs), 1))
    counts = mm(ones_where(onehot), before)
    place = jnp.sum(jnp.where(onehot, counts, 0.0), axis=0, keepdims=True).astype(jnp.int32)
    target = owner * SLOTS + place
    target_b = (owner % NZ) * zgrp + (owner // NZ) * SLOTS + place
    slot_row = iota((rows, docs), 0)
    pick_a = ones_where(slot_row == target)
    pick_b = ones_where(slot_row == target_b)
    prio = pi[...]
    line = iota((docs, docs), 0)
    meta = jnp.where(
        line == 0, su[...] + 1, jnp.where(line == 1, prio // 256, jnp.where(line == 2, prio % 256, 0))
    ).astype(jnp.float32).astype(jnp.bfloat16)
    r_i, c_i = iota((rows, rows), 0), iota((rows, rows), 1)
    y_bits, z_bits = NY.bit_length() - 1, NZ.bit_length() - 1
    slot, pair = r_i & 1, r_i >> 1
    to_z = ones_where(c_i == ((pair & (NY - 1)) * ygrp + (pair >> y_bits) * SLOTS + slot))
    to_y = ones_where(c_i == ((pair & (NZ - 1)) * zgrp + (pair >> z_bits) * SLOTS + slot))

    s1a[:, :meta_w] = mm_nt(pick_a, meta).astype(jnp.bfloat16)

    projected = jnp.zeros((docs, width), jnp.float32)
    for i in range(LOADS):
        loads[3 + 2 * i].wait()
        loads[4 + 2 * i].wait()
        projected += mm(st[:, i * step : (i + 1) * step], pr[i * step : (i + 1) * step, :])
    square_sum = jnp.sum(projected * projected, axis=1, keepdims=True)
    emb = (projected * lax.rsqrt(square_sum + 1e-06)).astype(jnp.bfloat16)

    sent = []

    def start(c):
        c.start()
        sent.append(c)
        return c

    def arrive(copies):
        for c in copies:
            c.wait_recv()

    def over_y(src, dst, cols, ssem, rsem):
        lanes = pl.ds(*cols)
        copies = [
            start(copy(src.at[yrows(y_at(i)), lanes], dst.at[yrows(my_y), lanes], ssem, rsem, i, y_dev(i)))
            for i in Y_FAR
        ]
        dst[yrows(my_y), lanes] = src[yrows(my_y), lanes]
        return copies

    def over_z(src, dst, cols, ssem, rsem):
        lanes = pl.ds(*cols)
        copies = [
            start(copy(src.at[zrows(z_at(j)), lanes], dst.at[zrows(my_z), lanes], ssem, rsem, j, z_dev(j)))
            for j in Z_FAR
        ]
        dst[zrows(my_z), lanes] = src[zrows(my_z), lanes]
        return copies

    def order(perm, src, dst, cols):
        lanes = pl.ds(*cols)
        dst[:, lanes] = mm(perm, src[:, lanes]).astype(jnp.bfloat16)

    a1, b1_, a2, b2_ = [], [], [], []
    for n in range(parts):
        at, size = x_cols[n]
        s1b[:, at : at + size] = mm(pick_b, emb[:, half + at : half + at + size]).astype(jnp.bfloat16)
        s1a[:, meta_w + at : meta_w + at + size] = mm(pick_a, emb[:, at : at + size]).astype(jnp.bfloat16)
        if n == 0:
            pl.semaphore_wait(barrier, NY + NZ + NG - 3)
        b1_.append(over_z(s1b, r1b, x_cols[n], z1s.at[n], z1r.at[n]))
        a1.append(over_y(s1a, r1a, a_cols[n], y1s.at[n], y1r.at[n]))
    for n in range(parts):
        arrive(b1_[n])
        order(to_y, r1b, s2b, x_cols[n])
        b2_.append(over_y(s2b, r2b, x_cols[n], y2s.at[n], y2r.at[n]))
        arrive(a1[n])
        order(to_z, r1a, s2a, a_cols[n])
        a2.append(over_z(s2a, r2a, a_cols[n], z2s.at[n], z2r.at[n]))

    up, down = g_dev(1), g_dev(NG - 1)

    def spread(src, dst, first, cols, base):
        to = pl.ds(*cols)
        frm = pl.ds(cols[0] + first, cols[1])
        c1 = start(copy(src.at[:, frm], dst.at[0, :, to], xs, xr, base, up))
        c2 = start(copy(src.at[:, frm], dst.at[1, :, to], xs, xr, base + 1, down))
        return c1, c2

    def onward(dst, held, cols, base, dev):
        to = pl.ds(*cols)
        return start(copy(dst.at[held, :, to], dst.at[2, :, to], xs, xr, base + 2, dev))

    w_row = iota((128, 128), 0)
    w_col = iota((128, 128), 1)

    def weights(at):
        return jnp.where(
            at == 0, 65536.0, jnp.where(at == 1, 256.0, jnp.where(at == 2, 1.0, 0.0))
        ).astype(jnp.bfloat16)

    xas, xbs, fas, fbs = [], [], [], []

    def forward_b(n):
        xbs[n][1].wait_recv()
        fbs.append(onward(xb, 1, x_cols[n], 6 * n, down))

    def forward_a(n):
        xas[n][0].wait_recv()
        fas.append(onward(xa, 0, x_cols[n], 6 * n + 3, up))

    for n in range(parts):
        arrive(b2_[n])
        xbs.append(spread(r2b, xb, 0, x_cols[n], 6 * n))
        if n:
            forward_b(n - 1)
        arrive(a2[n])
        xas.append(spread(r2a, xa, meta_w, x_cols[n], 6 * n + 3))
        if n:
            forward_a(n - 1)
        else:
            qmeta = r2a[:, :meta_w]
            krow[...] = mm_nt(weights(w_col)[:16], qmeta)[:8] - 65536.0
            kx = [
                start(copy(krow, xk.at[i - 1], xs, xr, 6 * parts + i - 1, g_dev(i)))
                for i in range(1, NG)
            ]
    forward_b(parts - 1)
    forward_a(parts - 1)
    qval = mm(qmeta, weights(w_row)) - 65536.0
    qbase = mm(qmeta, jnp.where(w_row == 0, 65536.0, 0.0).astype(jnp.bfloat16)) - 65536.0
    qa = r2a[:, meta_w:]
    qb = mm(to_z, r2b[...]).astype(jnp.bfloat16)

    def fold(acc, cosine, keys):
        for lane in range(0, rows, 128):
            key = keys[0:1, lane : lane + 128]
            ok = (key >= qbase) & (key < qval)
            acc = jnp.maximum(acc, jnp.where(ok, cosine[:, lane : lane + 128], -1.0))
        return acc

    def cosines(ka, kb):
        return mm_nt(qa, ka) + mm_nt(qb, mm(to_z, kb).astype(jnp.bfloat16))

    acc = fold(jnp.full((rows, 128), -1.0, jnp.float32), mm_nt(qa, qa) + mm_nt(qb, qb), krow[...])
    arrive(kx)
    arrive([c[0] for c in xbs])
    acc = fold(acc, cosines(xa[0], xb[0]), xk[0])
    arrive([c[1] for c in xas])
    acc = fold(acc, cosines(xa[1], xb[1]), xk[2])
    last = jnp.zeros((rows, rows), jnp.float32)
    for n in range(parts):
        cut = slice(x_cols[n][0], sum(x_cols[n]))
        fbs[n].wait_recv()
        last += mm_nt(qb[:, cut], mm(to_z, xb[2, :, cut]).astype(jnp.bfloat16))
        fas[n].wait_recv()
        last += mm_nt(qa[:, cut], xa[2, :, cut])
    acc = fold(acc, last, xk[1])

    best = jnp.max(jnp.transpose(acc), axis=0, keepdims=True)
    per = 128 // zgrp
    for h in range(rows // 128):
        sc[h] = best[:, h * 128 : (h + 1) * 128]
    b1, b2 = [], []
    for j in Z_FAR:
        c = copy(sc.at[z_at(j) // per], sr.at[my_z], b1s, b1r, j, z_dev(j))
        b1.append(start(c))
    sr[my_z] = sc[my_z // per]
    rb[...] = jnp.zeros_like(rb)
    for c in b1:
        c.wait_recv()
    for z in range(NZ):
        rb[z : z + 1, :] = sr[z]
    tb[...] = jnp.transpose(rb[...])

    def back_rows(y):
        return pl.ds(pl.multiple_of((my_z % per) * zgrp + (y // 4) * 8, 8), 8)

    for i in Y_FAR:
        c = copy(tb.at[back_rows(y_at(i)), :], rr.at[my_y], b2s, b2r, i, y_dev(i))
        b2.append(start(c))
    rr[my_y] = tb[back_rows(my_y), :]
    target_col = jnp.transpose(jnp.broadcast_to(target.astype(jnp.float32), (docs, docs)))
    lanes = iota((1, 128), 1)
    res = jnp.full((docs, 128), -2.0, jnp.float32)
    for c in sent[: -len(b2)]:
        c.wait_send()
    for c in b2:
        c.wait_recv()
    for y in range(NY):
        for s in range(SLOTS):
            score = rr[y, pl.ds((my_y % 4) * SLOTS + s, 1), :]
            code = jnp.where(lanes < NZ, (y * NZ + lanes) * SLOTS + s, -1).astype(jnp.float32)
            res = jnp.where(target_col == code, score, res)
    out[...] = jnp.max(jnp.transpose(res), axis=0, keepdims=True)

    for c in b2:
        c.wait_send()


def on_device(states, projection, owner_group, cluster_sub, priority):
    docs = states.shape[0]
    width = projection.shape[1]
    half = width // 2
    parts = PARTS
    rows = NY * NZ * SLOTS
    bf, f32 = jnp.bfloat16, jnp.float32
    vmem = pl.BlockSpec(memory_space=pltpu.VMEM)
    dma = pltpu.SemaphoreType.DMA
    score = pl.pallas_call(
        kernel,
        out_shape=jax.ShapeDtypeStruct((1, docs), f32),
        in_specs=[pl.BlockSpec(memory_space=pltpu.HBM)] * 5,
        out_specs=vmem,
        scratch_shapes=[
            pltpu.VMEM(states.shape, bf),
            pltpu.VMEM(projection.shape, bf),
            pltpu.VMEM((1, docs), jnp.int32),
            pltpu.VMEM((1, docs), jnp.int32),
            pltpu.VMEM((1, docs), jnp.int32),
            dma((3 + 2 * LOADS,)),
            pltpu.VMEM((rows, half + 128), bf),
            pltpu.VMEM((rows, half), bf),
            pltpu.VMEM((rows, half + 128), bf),
            pltpu.VMEM((rows, half), bf),
            pltpu.VMEM((rows, half + 128), bf),
            pltpu.VMEM((rows, half), bf),
            pltpu.VMEM((rows, half + 128), bf),
            pltpu.VMEM((rows, half), bf),
            pltpu.VMEM((8, rows), f32),
            pltpu.VMEM((3, rows, half), bf),
            pltpu.VMEM((3, rows, half), bf),
            pltpu.VMEM((3, 8, rows), f32),
            pltpu.VMEM((rows // 128, 1, 128), f32),
            pltpu.VMEM((NZ, 1, 128), f32),
            pltpu.VMEM((128, 128), f32),
            pltpu.VMEM((128, 128), f32),
            pltpu.VMEM((NY, 8, 128), f32),
            dma((parts, NY)), dma((parts, NY)), dma((parts, NZ)), dma((parts, NZ)),
            dma((parts, NZ)), dma((parts, NZ)), dma((parts, NY)), dma((parts, NY)),
            dma((6 * parts + NG - 1,)), dma((6 * parts + NG - 1,)),
            dma((NZ,)), dma((NZ,)), dma((NY,)), dma((NY,)),
        ],
        compiler_params=pltpu.CompilerParams(
            collective_id=0, has_side_effects=True, vmem_limit_bytes=67043328
        ),
    )(
        states,
        projection,
        owner_group.reshape(1, docs),
        cluster_sub.reshape(1, docs),
        priority.reshape(1, docs),
    )
    return score.reshape(docs)


def solution(mesh):
    in_specs = (
        P(("dp", "grp"), None),
        P(),
        P(("dp", "grp"), None),
        P(("dp", "grp")),
        P(("dp", "grp")),
    )
    return jax.shard_map(
        on_device, mesh=mesh, in_specs=in_specs, out_specs=P(("dp", "grp")), check_vma=False
    )
```

```python
import functools

import jax
import jax.numpy as jnp
from jax import lax
from jax.experimental import pallas as pl
from jax.experimental.pallas import tpu as pltpu
from jax.sharding import PartitionSpec as P

MESH = pl.DeviceIdType.MESH
NY = 8
NZ = 16
NG = 4
SLOTS = 2
LOADS = 2
CUTS = (0, 1, 3)
PARTS = len(CUTS) - 1
LAG = 2
NT = (((1,), (1,)), ((), ()))
Y_FAR = sorted(range(1, NY), key=lambda i: -min(i, NY - i))
Z_FAR = sorted(range(1, NZ), key=lambda j: -min(j, NZ - j))


def mm(a, b):
    return jnp.dot(a, b, preferred_element_type=jnp.float32)


def mm_nt(a, b):
    return lax.dot_general(a, b, NT, preferred_element_type=jnp.float32)


def iota(shape, axis):
    return lax.broadcasted_iota(jnp.int32, shape, axis)


def ones_where(cond):
    return jnp.where(cond, 1.0, 0.0).astype(jnp.bfloat16)


def kernel(
    st_hbm, pr_hbm, ow_hbm, su_hbm, pi_hbm, out,
    st, pr, ow, su, pi, load,
    s1a, s1b, r1a, r1b, s2a, s2b, r2a, r2b,
    krow, xa, xb, xk, sc, sr, rb, tb, rr,
    y1s, y1r, z1s, z1r, z2s, z2r, y2s, y2r, xs, xr, b1s, b1r, b2s, b2r,
):
    docs = st.shape[0]
    depth, width = pr.shape
    half = width // 2
    meta_w = s1a.shape[1] - half
    parts = PARTS
    x_cols = [(lo * 128, (hi - lo) * 128) for lo, hi in zip(CUTS[:-1], CUTS[1:])]
    a_cols = [(meta_w + at if at else 0, size if at else meta_w + size) for at, size in x_cols]
    step = depth // LOADS
    rows = NY * NZ * SLOTS
    ygrp = NZ * SLOTS
    zgrp = NY * SLOTS
    dp = lax.axis_index("dp")
    grp = lax.axis_index("grp")
    my_y = dp // NZ
    my_z = dp % NZ

    def y_at(i):
        return (my_y + i) % NY

    def z_at(j):
        return (my_z + j) % NZ

    def g_at(i):
        return (grp + i) % NG

    def y_dev(i):
        return {"dp": y_at(i) * NZ + my_z}

    def z_dev(j):
        return {"dp": my_y * NZ + z_at(j)}

    def g_dev(i):
        return {"grp": g_at(i)}

    def copy(src, dst, ssem, rsem, i, dev):
        return pltpu.make_async_remote_copy(
            src_ref=src, dst_ref=dst, send_sem=ssem.at[i], recv_sem=rsem.at[i],
            device_id=dev, device_id_type=MESH,
        )

    def yrows(y):
        return pl.ds(pl.multiple_of(y * ygrp, ygrp), ygrp)

    def zrows(z):
        return pl.ds(pl.multiple_of(z * zgrp, zgrp), zgrp)

    barrier = pltpu.get_barrier_semaphore()
    for i in range(1, NY):
        pl.semaphore_signal(barrier, inc=1, device_id=y_dev(i), device_id_type=MESH)
    for j in range(1, NZ):
        pl.semaphore_signal(barrier, inc=1, device_id=z_dev(j), device_id_type=MESH)
    for i in range(1, NG):
        pl.semaphore_signal(barrier, inc=1, device_id=g_dev(i), device_id_type=MESH)

    loads = []
    for i, (src, dst) in enumerate(((ow_hbm, ow), (su_hbm, su), (pi_hbm, pi))):
        loads.append(pltpu.make_async_copy(src, dst, load.at[i]))
    for i in range(LOADS):
        cut = pl.ds(i * step, step)
        loads.append(pltpu.make_async_copy(st_hbm.at[:, cut], st.at[:, cut], load.at[3 + 2 * i]))
        loads.append(pltpu.make_async_copy(pr_hbm.at[cut, :], pr.at[cut, :], load.at[4 + 2 * i]))
    for c in loads:
        c.start()
    for c in loads[:3]:
        c.wait()
    owner = ow[...]
    onehot = iota((NY * NZ, docs), 0) == owner
    before = ones_where(iota((docs, docs), 0) < iota((docs, docs), 1))
    counts = mm(ones_where(onehot), before)
    place = jnp.sum(jnp.where(onehot, counts, 0.0), axis=0, keepdims=True).astype(jnp.int32)
    target = owner * SLOTS + place
    target_b = (owner % NZ) * zgrp + (owner // NZ) * SLOTS + place
    slot_row = iota((rows, docs), 0)
    pick_a = ones_where(slot_row == target)
    pick_b = ones_where(slot_row == target_b)
    prio = pi[...]
    line = iota((docs, docs), 0)
    meta = jnp.where(
        line == 0, su[...] + 1, jnp.where(line == 1, prio // 256, jnp.where(line == 2, prio % 256, 0))
    ).astype(jnp.float32).astype(jnp.bfloat16)
    r_i, c_i = iota((rows, rows), 0), iota((rows, rows), 1)
    y_bits, z_bits = NY.bit_length() - 1, NZ.bit_length() - 1
    slot, pair = r_i & 1, r_i >> 1
    to_z = ones_where(c_i == ((pair & (NY - 1)) * ygrp + (pair >> y_bits) * SLOTS + slot))
    to_y = ones_where(c_i == ((pair & (NZ - 1)) * zgrp + (pair >> z_bits) * SLOTS + slot))

    s1a[:, :meta_w] = mm_nt(pick_a, meta).astype(jnp.bfloat16)

    projected = jnp.zeros((docs, width), jnp.float32)
    for i in range(LOADS):
        loads[3 + 2 * i].wait()
        loads[4 + 2 * i].wait()
        projected += mm(st[:, i * step : (i + 1) * step], pr[i * step : (i + 1) * step, :])
    square_sum = jnp.sum(projected * projected, axis=1, keepdims=True)
    emb = (projected * lax.rsqrt(square_sum + 1e-06)).astype(jnp.bfloat16)

    sent = []

    def start(c):
        c.start()
        sent.append(c)
        return c

    def arrive(copies):
        for c in copies:
            c.wait_recv()

    def over_y(src, dst, cols, ssem, rsem):
        lanes = pl.ds(*cols)
        copies = [
            start(copy(src.at[yrows(y_at(i)), lanes], dst.at[yrows(my_y), lanes], ssem, rsem, i, y_dev(i)))
            for i in Y_FAR
        ]
        dst[yrows(my_y), lanes] = src[yrows(my_y), lanes]
        return copies

    def over_z(src, dst, cols, ssem, rsem):
        lanes = pl.ds(*cols)
        copies = [
            start(copy(src.at[zrows(z_at(j)), lanes], dst.at[zrows(my_z), lanes], ssem, rsem, j, z_dev(j)))
            for j in Z_FAR
        ]
        dst[zrows(my_z), lanes] = src[zrows(my_z), lanes]
        return copies

    def order(perm, src, dst, cols):
        lanes = pl.ds(*cols)
        dst[:, lanes] = mm(perm, src[:, lanes]).astype(jnp.bfloat16)

    a1, b1_, a2, b2_ = [], [], [], []
    for n in range(parts):
        at, size = x_cols[n]
        s1b[:, at : at + size] = mm(pick_b, emb[:, half + at : half + at + size]).astype(jnp.bfloat16)
        s1a[:, meta_w + at : meta_w + at + size] = mm(pick_a, emb[:, at : at + size]).astype(jnp.bfloat16)
        if n == 0:
            pl.semaphore_wait(barrier, NY + NZ + NG - 3)
        b1_.append(over_z(s1b, r1b, x_cols[n], z1s.at[n], z1r.at[n]))
        a1.append(over_y(s1a, r1a, a_cols[n], y1s.at[n], y1r.at[n]))
    for n in range(parts):
        arrive(b1_[n])
        order(to_y, r1b, s2b, x_cols[n])
        b2_.append(over_y(s2b, r2b, x_cols[n], y2s.at[n], y2r.at[n]))
        arrive(a1[n])
        order(to_z, r1a, s2a, a_cols[n])
        a2.append(over_z(s2a, r2a, a_cols[n], z2s.at[n], z2r.at[n]))

    up, down = g_dev(1), g_dev(NG - 1)

    def spread(src, dst, first, cols, base):
        to = pl.ds(*cols)
        frm = pl.ds(cols[0] + first, cols[1])
        c1 = start(copy(src.at[:, frm], dst.at[0, :, to], xs, xr, base, up))
        c2 = start(copy(src.at[:, frm], dst.at[1, :, to], xs, xr, base + 1, down))
        return c1, c2

    def onward(dst, held, cols, base, dev):
        to = pl.ds(*cols)
        return start(copy(dst.at[held, :, to], dst.at[2, :, to], xs, xr, base + 2, dev))

    w_col = iota((128, 128), 1)

    def weights(at):
        return jnp.where(
            at == 0, 65536.0, jnp.where(at == 1, 256.0, jnp.where(at == 2, 1.0, 0.0))
        ).astype(jnp.bfloat16)

    xas, xbs, fas, fbs = [], [], [], []

    def forward_b(n):
        xbs[n][1].wait_recv()
        fbs.append(onward(xb, 1, x_cols[n], 6 * n, down))

    def forward_a(n):
        xas[n][0].wait_recv()
        fas.append(onward(xa, 0, x_cols[n], 6 * n + 3, up))

    for n in range(parts):
        arrive(b2_[n])
        xbs.append(spread(r2b, xb, 0, x_cols[n], 6 * n))
        if n >= LAG:
            forward_b(n - LAG)
        arrive(a2[n])
        xas.append(spread(r2a, xa, meta_w, x_cols[n], 6 * n + 3))
        if n >= LAG:
            forward_a(n - LAG)
        if n == 0:
            qmeta = r2a[:, :meta_w]
            krow[...] = mm_nt(weights(w_col)[:16], qmeta)[:8] - 65536.0
            kx = [
                start(copy(krow, xk.at[i - 1], xs, xr, 6 * parts + i - 1, g_dev(i)))
                for i in range(1, NG)
            ]
            qval = krow[0:1, :]
            whole = jnp.where(w_col == 0, 65536.0, 0.0).astype(jnp.bfloat16)
            qbase = mm_nt(whole[:16], qmeta)[0:1] - 65536.0
    for n in range(max(0, parts - LAG), parts):
        forward_b(n)
        forward_a(n)
    qa = r2a[:, meta_w:]
    qb = mm(to_z, r2b[...]).astype(jnp.bfloat16)

    def column(keys):
        tiles = [jnp.broadcast_to(keys[0:1, at : at + 128], (128, 128)) for at in range(0, rows, 128)]
        return jnp.concatenate([jnp.transpose(t) for t in tiles], axis=0)

    def fold(best, cosine, keys):
        found = []
        for h, old in enumerate(best):
            cut = slice(h * 128, (h + 1) * 128)
            ok = (keys >= qbase[:, cut]) & (keys < qval[:, cut])
            top = jnp.max(jnp.where(ok, cosine[:, cut], -1.0), axis=0, keepdims=True)
            found.append(jnp.maximum(old, top))
        return found

    def cosines(ka, kb):
        return mm_nt(ka, qa) + mm_nt(mm(to_z, kb).astype(jnp.bfloat16), qb)

    best = [jnp.full((1, 128), -1.0, jnp.float32)] * (rows // 128)
    best = fold(best, mm_nt(qa, qa) + mm_nt(qb, qb), column(krow[...]))
    arrive(kx)
    keys = [column(xk[i]) for i in range(NG - 1)]
    arrive([c[0] for c in xbs])
    best = fold(best, cosines(xa[0], xb[0]), keys[0])
    arrive([c[1] for c in xas])
    best = fold(best, cosines(xa[1], xb[1]), keys[2])
    last = jnp.zeros((rows, rows), jnp.float32)
    for n in range(parts):
        cut = slice(x_cols[n][0], sum(x_cols[n]))
        fbs[n].wait_recv()
        last += mm_nt(mm(to_z, xb[2, :, cut]).astype(jnp.bfloat16), qb[:, cut])
        fas[n].wait_recv()
        last += mm_nt(xa[2, :, cut], qa[:, cut])
    best = fold(best, last, keys[1])

    per = 128 // zgrp
    for h in range(rows // 128):
        sc[h] = best[h]
    b1, b2 = [], []
    for j in Z_FAR:
        c = copy(sc.at[z_at(j) // per], sr.at[my_z], b1s, b1r, j, z_dev(j))
        b1.append(start(c))
    sr[my_z] = sc[my_z // per]
    rb[...] = jnp.zeros_like(rb)
    for c in b1:
        c.wait_recv()
    for z in range(NZ):
        rb[z : z + 1, :] = sr[z]
    tb[...] = jnp.transpose(rb[...])

    def back_rows(y):
        return pl.ds(pl.multiple_of((my_z % per) * zgrp + (y // 4) * 8, 8), 8)

    for i in Y_FAR:
        c = copy(tb.at[back_rows(y_at(i)), :], rr.at[my_y], b2s, b2r, i, y_dev(i))
        b2.append(start(c))
    rr[my_y] = tb[back_rows(my_y), :]
    target_col = jnp.transpose(jnp.broadcast_to(target.astype(jnp.float32), (docs, docs)))
    lanes = iota((1, 128), 1)
    res = jnp.full((docs, 128), -2.0, jnp.float32)
    for c in sent[: -len(b2)]:
        c.wait_send()
    for c in b2:
        c.wait_recv()
    for y in range(NY):
        for s in range(SLOTS):
            score = rr[y, pl.ds((my_y % 4) * SLOTS + s, 1), :]
            code = jnp.where(lanes < NZ, (y * NZ + lanes) * SLOTS + s, -1).astype(jnp.float32)
            res = jnp.where(target_col == code, score, res)
    out[...] = jnp.max(jnp.transpose(res), axis=0, keepdims=True)

    for c in b2:
        c.wait_send()


def on_device(states, projection, owner_group, cluster_sub, priority):
    docs = states.shape[0]
    width = projection.shape[1]
    half = width // 2
    parts = PARTS
    rows = NY * NZ * SLOTS
    bf, f32 = jnp.bfloat16, jnp.float32
    vmem = pl.BlockSpec(memory_space=pltpu.VMEM)
    dma = pltpu.SemaphoreType.DMA
    score = pl.pallas_call(
        kernel,
        out_shape=jax.ShapeDtypeStruct((1, docs), f32),
        in_specs=[pl.BlockSpec(memory_space=pltpu.HBM)] * 5,
        out_specs=vmem,
        scratch_shapes=[
            pltpu.VMEM(states.shape, bf),
            pltpu.VMEM(projection.shape, bf),
            pltpu.VMEM((1, docs), jnp.int32),
            pltpu.VMEM((1, docs), jnp.int32),
            pltpu.VMEM((1, docs), jnp.int32),
            dma((3 + 2 * LOADS,)),
            pltpu.VMEM((rows, half + 128), bf),
            pltpu.VMEM((rows, half), bf),
            pltpu.VMEM((rows, half + 128), bf),
            pltpu.VMEM((rows, half), bf),
            pltpu.VMEM((rows, half + 128), bf),
            pltpu.VMEM((rows, half), bf),
            pltpu.VMEM((rows, half + 128), bf),
            pltpu.VMEM((rows, half), bf),
            pltpu.VMEM((8, rows), f32),
            pltpu.VMEM((3, rows, half), bf),
            pltpu.VMEM((3, rows, half), bf),
            pltpu.VMEM((3, 8, rows), f32),
            pltpu.VMEM((rows // 128, 1, 128), f32),
            pltpu.VMEM((NZ, 1, 128), f32),
            pltpu.VMEM((128, 128), f32),
            pltpu.VMEM((128, 128), f32),
            pltpu.VMEM((NY, 8, 128), f32),
            dma((parts, NY)), dma((parts, NY)), dma((parts, NZ)), dma((parts, NZ)),
            dma((parts, NZ)), dma((parts, NZ)), dma((parts, NY)), dma((parts, NY)),
            dma((6 * parts + NG - 1,)), dma((6 * parts + NG - 1,)),
            dma((NZ,)), dma((NZ,)), dma((NY,)), dma((NY,)),
        ],
        compiler_params=pltpu.CompilerParams(
            collective_id=0, has_side_effects=True, vmem_limit_bytes=48 * 1024 * 1024
        ),
    )(
        *(
            pltpu.with_memory_space_constraint(x, pltpu.HBM)
            for x in (
                states,
                projection,
                owner_group.reshape(1, docs),
                cluster_sub.reshape(1, docs),
                priority.reshape(1, docs),
            )
        ),
    )
    return score.reshape(docs)


def solution(mesh):
    in_specs = (
        P(("dp", "grp"), None),
        P(),
        P(("dp", "grp"), None),
        P(("dp", "grp")),
        P(("dp", "grp")),
    )
    return jax.shard_map(
        on_device, mesh=mesh, in_specs=in_specs, out_specs=P(("dp", "grp")), check_vma=False
    )
```

```python
import functools

import jax
import jax.numpy as jnp
from jax import lax
from jax.experimental import pallas as pl
from jax.experimental.pallas import tpu as pltpu
from jax.sharding import PartitionSpec as P

MESH = pl.DeviceIdType.MESH
NY = 8
NZ = 16
NG = 4
SLOTS = 2
LOADS = 2
CUTS = (0, 1, 3)
PARTS = len(CUTS) - 1
LAG = 2
NT = (((1,), (1,)), ((), ()))
Y_FAR = sorted(range(1, NY), key=lambda i: -min(i, NY - i))
Z_FAR = sorted(range(1, NZ), key=lambda j: -min(j, NZ - j))


def mm(a, b):
    return jnp.dot(a, b, preferred_element_type=jnp.float32)


def mm_nt(a, b):
    return lax.dot_general(a, b, NT, preferred_element_type=jnp.float32)


def iota(shape, axis):
    return lax.broadcasted_iota(jnp.int32, shape, axis)


def ones_where(cond):
    return jnp.where(cond, 1.0, 0.0).astype(jnp.bfloat16)


def kernel(
    st_hbm, pr_hbm, ow_hbm, su_hbm, pi_hbm, out,
    st, pr, ow, su, pi, load,
    s1a, s1b, r1a, r1b, s2a, s2b, r2a, r2b,
    krow, xa, xb, xk, sc, sr, rb, tb, rr,
    y1s, y1r, z1s, z1r, z2s, z2r, y2s, y2r, xs, xr, b1s, b1r, b2s, b2r,
):
    docs = st.shape[0]
    depth, width = pr.shape
    half = width // 2
    meta_w = s1a.shape[1] - half
    parts = PARTS
    x_cols = [(lo * 128, (hi - lo) * 128) for lo, hi in zip(CUTS[:-1], CUTS[1:])]
    a_cols = [(meta_w + at if at else 0, size if at else meta_w + size) for at, size in x_cols]
    step = depth // LOADS
    rows = NY * NZ * SLOTS
    ygrp = NZ * SLOTS
    zgrp = NY * SLOTS
    dp = lax.axis_index("dp")
    grp = lax.axis_index("grp")
    my_y = dp // NZ
    my_z = dp % NZ

    def y_at(i):
        return (my_y + i) % NY

    def z_at(j):
        return (my_z + j) % NZ

    def g_at(i):
        return (grp + i) % NG

    def y_dev(i):
        return {"dp": y_at(i) * NZ + my_z}

    def z_dev(j):
        return {"dp": my_y * NZ + z_at(j)}

    def g_dev(i):
        return {"grp": g_at(i)}

    def copy(src, dst, ssem, rsem, i, dev):
        return pltpu.make_async_remote_copy(
            src_ref=src, dst_ref=dst, send_sem=ssem.at[i], recv_sem=rsem.at[i],
            device_id=dev, device_id_type=MESH,
        )

    def yrows(y):
        return pl.ds(pl.multiple_of(y * ygrp, ygrp), ygrp)

    def zrows(z):
        return pl.ds(pl.multiple_of(z * zgrp, zgrp), zgrp)

    barrier = pltpu.get_barrier_semaphore()
    for i in range(1, NY):
        pl.semaphore_signal(barrier, inc=1, device_id=y_dev(i), device_id_type=MESH)
    for j in range(1, NZ):
        pl.semaphore_signal(barrier, inc=1, device_id=z_dev(j), device_id_type=MESH)
    for i in range(1, NG):
        pl.semaphore_signal(barrier, inc=1, device_id=g_dev(i), device_id_type=MESH)

    loads = []
    for i, (src, dst) in enumerate(((ow_hbm, ow), (su_hbm, su), (pi_hbm, pi))):
        loads.append(pltpu.make_async_copy(src, dst, load.at[i]))
    for i in range(LOADS):
        cut = pl.ds(i * step, step)
        loads.append(pltpu.make_async_copy(st_hbm.at[:, cut], st.at[:, cut], load.at[3 + 2 * i]))
        loads.append(pltpu.make_async_copy(pr_hbm.at[cut, :], pr.at[cut, :], load.at[4 + 2 * i]))
    for c in loads:
        c.start()
    for c in loads[:3]:
        c.wait()
    owner = ow[...]
    onehot = iota((NY * NZ, docs), 0) == owner
    before = ones_where(iota((docs, docs), 0) < iota((docs, docs), 1))
    counts = mm(ones_where(onehot), before)
    place = jnp.sum(jnp.where(onehot, counts, 0.0), axis=0, keepdims=True).astype(jnp.int32)
    target = owner * SLOTS + place
    target_b = (owner % NZ) * zgrp + (owner // NZ) * SLOTS + place
    slot_row = iota((rows, docs), 0)
    pick_a = ones_where(slot_row == target)
    pick_b = ones_where(slot_row == target_b)
    prio = pi[...]
    line = iota((docs, docs), 0)
    meta = jnp.where(
        line == 0, su[...] + 1, jnp.where(line == 1, prio // 256, jnp.where(line == 2, prio % 256, 0))
    ).astype(jnp.float32).astype(jnp.bfloat16)
    r_i, c_i = iota((rows, rows), 0), iota((rows, rows), 1)
    y_bits, z_bits = NY.bit_length() - 1, NZ.bit_length() - 1
    slot, pair = r_i & 1, r_i >> 1
    to_z = ones_where(c_i == ((pair & (NY - 1)) * ygrp + (pair >> y_bits) * SLOTS + slot))
    to_y = ones_where(c_i == ((pair & (NZ - 1)) * zgrp + (pair >> z_bits) * SLOTS + slot))

    s1a[:, :meta_w] = mm_nt(pick_a, meta).astype(jnp.bfloat16)

    projected = jnp.zeros((docs, width), jnp.float32)
    for i in range(LOADS):
        loads[3 + 2 * i].wait()
        loads[4 + 2 * i].wait()
        projected += mm(st[:, i * step : (i + 1) * step], pr[i * step : (i + 1) * step, :])
    square_sum = jnp.sum(projected * projected, axis=1, keepdims=True)
    emb = (projected * lax.rsqrt(square_sum + 1e-06)).astype(jnp.bfloat16)

    sent = []

    def start(c):
        c.start()
        sent.append(c)
        return c

    def arrive(copies):
        for c in copies:
            c.wait_recv()

    def over_y(src, dst, cols, ssem, rsem):
        lanes = pl.ds(*cols)
        copies = [
            start(copy(src.at[yrows(y_at(i)), lanes], dst.at[yrows(my_y), lanes], ssem, rsem, i, y_dev(i)))
            for i in Y_FAR
        ]
        dst[yrows(my_y), lanes] = src[yrows(my_y), lanes]
        return copies

    def over_z(src, dst, cols, ssem, rsem):
        lanes = pl.ds(*cols)
        copies = [
            start(copy(src.at[zrows(z_at(j)), lanes], dst.at[zrows(my_z), lanes], ssem, rsem, j, z_dev(j)))
            for j in Z_FAR
        ]
        dst[zrows(my_z), lanes] = src[zrows(my_z), lanes]
        return copies

    def order(perm, src, dst, cols):
        lanes = pl.ds(*cols)
        dst[:, lanes] = mm(perm, src[:, lanes]).astype(jnp.bfloat16)

    a1, b1_, a2, b2_ = [], [], [], []
    for n in range(parts):
        at, size = x_cols[n]
        s1b[:, at : at + size] = mm(pick_b, emb[:, half + at : half + at + size]).astype(jnp.bfloat16)
        s1a[:, meta_w + at : meta_w + at + size] = mm(pick_a, emb[:, at : at + size]).astype(jnp.bfloat16)
        if n == 0:
            pl.semaphore_wait(barrier, NY + NZ + NG - 3)
        a1.append(over_y(s1a, r1a, a_cols[n], y1s.at[n], y1r.at[n]))
        b1_.append(over_z(s1b, r1b, x_cols[n], z1s.at[n], z1r.at[n]))
    for n in range(parts):
        arrive(b1_[n])
        order(to_y, r1b, s2b, x_cols[n])
        b2_.append(over_y(s2b, r2b, x_cols[n], y2s.at[n], y2r.at[n]))
        arrive(a1[n])
        order(to_z, r1a, s2a, a_cols[n])
        a2.append(over_z(s2a, r2a, a_cols[n], z2s.at[n], z2r.at[n]))

    up, down = g_dev(1), g_dev(NG - 1)

    def spread(src, dst, first, cols, base):
        to = pl.ds(*cols)
        frm = pl.ds(cols[0] + first, cols[1])
        c1 = start(copy(src.at[:, frm], dst.at[0, :, to], xs, xr, base, up))
        c2 = start(copy(src.at[:, frm], dst.at[1, :, to], xs, xr, base + 1, down))
        return c1, c2

    def onward(dst, held, cols, base, dev):
        to = pl.ds(*cols)
        return start(copy(dst.at[held, :, to], dst.at[2, :, to], xs, xr, base + 2, dev))

    w_col = iota((128, 128), 1)

    def weights(at):
        return jnp.where(
            at == 0, 65536.0, jnp.where(at == 1, 256.0, jnp.where(at == 2, 1.0, 0.0))
        ).astype(jnp.bfloat16)

    xas, xbs, fas, fbs = [], [], [], []

    def forward_b(n):
        xbs[n][1].wait_recv()
        fbs.append(onward(xb, 1, x_cols[n], 6 * n, down))

    def forward_a(n):
        xas[n][0].wait_recv()
        fas.append(onward(xa, 0, x_cols[n], 6 * n + 3, up))

    for n in range(parts):
        arrive(b2_[n])
        xbs.append(spread(r2b, xb, 0, x_cols[n], 6 * n))
        if n >= LAG:
            forward_b(n - LAG)
        arrive(a2[n])
        xas.append(spread(r2a, xa, meta_w, x_cols[n], 6 * n + 3))
        if n >= LAG:
            forward_a(n - LAG)
        if n == 0:
            qmeta = r2a[:, :meta_w]
            krow[...] = mm_nt(weights(w_col)[:16], qmeta)[:8] - 65536.0
            kx = [
                start(copy(krow, xk.at[i - 1], xs, xr, 6 * parts + i - 1, g_dev(i)))
                for i in range(1, NG)
            ]
            qval = krow[0:1, :]
            whole = jnp.where(w_col == 0, 65536.0, 0.0).astype(jnp.bfloat16)
            qbase = mm_nt(whole[:16], qmeta)[0:1] - 65536.0
    for n in range(max(0, parts - LAG), parts):
        forward_b(n)
        forward_a(n)
    qa = r2a[:, meta_w:]
    qb = mm(to_z, r2b[...]).astype(jnp.bfloat16)

    def column(keys):
        tiles = [jnp.broadcast_to(keys[0:1, at : at + 128], (128, 128)) for at in range(0, rows, 128)]
        return jnp.concatenate([jnp.transpose(t) for t in tiles], axis=0)

    def fold(best, cosine, keys):
        found = []
        for h, old in enumerate(best):
            cut = slice(h * 128, (h + 1) * 128)
            ok = (keys >= qbase[:, cut]) & (keys < qval[:, cut])
            top = jnp.max(jnp.where(ok, cosine[:, cut], -1.0), axis=0, keepdims=True)
            found.append(jnp.maximum(old, top))
        return found

    def cosines(ka, kb):
        return mm_nt(ka, qa) + mm_nt(mm(to_z, kb).astype(jnp.bfloat16), qb)

    best = [jnp.full((1, 128), -1.0, jnp.float32)] * (rows // 128)
    best = fold(best, mm_nt(qa, qa) + mm_nt(qb, qb), column(krow[...]))
    arrive(kx)
    keys = [column(xk[i]) for i in range(NG - 1)]
    arrive([c[0] for c in xbs])
    best = fold(best, cosines(xa[0], xb[0]), keys[0])
    arrive([c[1] for c in xas])
    best = fold(best, cosines(xa[1], xb[1]), keys[2])
    last = jnp.zeros((rows, rows), jnp.float32)
    for n in range(parts):
        cut = slice(x_cols[n][0], sum(x_cols[n]))
        fbs[n].wait_recv()
        last += mm_nt(mm(to_z, xb[2, :, cut]).astype(jnp.bfloat16), qb[:, cut])
        fas[n].wait_recv()
        last += mm_nt(xa[2, :, cut], qa[:, cut])
    best = fold(best, last, keys[1])

    per = 128 // zgrp
    for h in range(rows // 128):
        sc[h] = best[h]
    b1, b2 = [], []
    for j in Z_FAR:
        c = copy(sc.at[z_at(j) // per], sr.at[my_z], b1s, b1r, j, z_dev(j))
        b1.append(start(c))
    sr[my_z] = sc[my_z // per]
    rb[...] = jnp.zeros_like(rb)
    for c in b1:
        c.wait_recv()
    for z in range(NZ):
        rb[z : z + 1, :] = sr[z]
    tb[...] = jnp.transpose(rb[...])

    def back_rows(y):
        return pl.ds(pl.multiple_of((my_z % per) * zgrp + (y // 4) * 8, 8), 8)

    for i in Y_FAR:
        c = copy(tb.at[back_rows(y_at(i)), :], rr.at[my_y], b2s, b2r, i, y_dev(i))
        b2.append(start(c))
    rr[my_y] = tb[back_rows(my_y), :]
    target_col = jnp.transpose(jnp.broadcast_to(target.astype(jnp.float32), (docs, docs)))
    lanes = iota((1, 128), 1)
    res = jnp.full((docs, 128), -2.0, jnp.float32)
    for c in sent[: -len(b2)]:
        c.wait_send()
    for c in b2:
        c.wait_recv()
    for y in range(NY):
        for s in range(SLOTS):
            score = rr[y, pl.ds((my_y % 4) * SLOTS + s, 1), :]
            code = jnp.where(lanes < NZ, (y * NZ + lanes) * SLOTS + s, -1).astype(jnp.float32)
            res = jnp.where(target_col == code, score, res)
    out[...] = jnp.max(jnp.transpose(res), axis=0, keepdims=True)

    for c in b2:
        c.wait_send()


def on_device(states, projection, owner_group, cluster_sub, priority):
    docs = states.shape[0]
    width = projection.shape[1]
    half = width // 2
    parts = PARTS
    rows = NY * NZ * SLOTS
    bf, f32 = jnp.bfloat16, jnp.float32
    vmem = pl.BlockSpec(memory_space=pltpu.VMEM)
    dma = pltpu.SemaphoreType.DMA
    score = pl.pallas_call(
        kernel,
        out_shape=jax.ShapeDtypeStruct((1, docs), f32),
        in_specs=[pl.BlockSpec(memory_space=pltpu.HBM)] * 5,
        out_specs=vmem,
        scratch_shapes=[
            pltpu.VMEM(states.shape, bf),
            pltpu.VMEM(projection.shape, bf),
            pltpu.VMEM((1, docs), jnp.int32),
            pltpu.VMEM((1, docs), jnp.int32),
            pltpu.VMEM((1, docs), jnp.int32),
            dma((3 + 2 * LOADS,)),
            pltpu.VMEM((rows, half + 128), bf),
            pltpu.VMEM((rows, half), bf),
            pltpu.VMEM((rows, half + 128), bf),
            pltpu.VMEM((rows, half), bf),
            pltpu.VMEM((rows, half + 128), bf),
            pltpu.VMEM((rows, half), bf),
            pltpu.VMEM((rows, half + 128), bf),
            pltpu.VMEM((rows, half), bf),
            pltpu.VMEM((8, rows), f32),
            pltpu.VMEM((3, rows, half), bf),
            pltpu.VMEM((3, rows, half), bf),
            pltpu.VMEM((3, 8, rows), f32),
            pltpu.VMEM((rows // 128, 1, 128), f32),
            pltpu.VMEM((NZ, 1, 128), f32),
            pltpu.VMEM((128, 128), f32),
            pltpu.VMEM((128, 128), f32),
            pltpu.VMEM((NY, 8, 128), f32),
            dma((parts, NY)), dma((parts, NY)), dma((parts, NZ)), dma((parts, NZ)),
            dma((parts, NZ)), dma((parts, NZ)), dma((parts, NY)), dma((parts, NY)),
            dma((6 * parts + NG - 1,)), dma((6 * parts + NG - 1,)),
            dma((NZ,)), dma((NZ,)), dma((NY,)), dma((NY,)),
        ],
        compiler_params=pltpu.CompilerParams(
            collective_id=0, has_side_effects=True, vmem_limit_bytes=48 * 1024 * 1024
        ),
    )(
        *(
            pltpu.with_memory_space_constraint(x, pltpu.HBM)
            for x in (
                states,
                projection,
                owner_group.reshape(1, docs),
                cluster_sub.reshape(1, docs),
                priority.reshape(1, docs),
            )
        ),
    )
    return score.reshape(docs)


def solution(mesh):
    in_specs = (
        P(("dp", "grp"), None),
        P(),
        P(("dp", "grp"), None),
        P(("dp", "grp")),
        P(("dp", "grp")),
    )
    return jax.shard_map(
        on_device, mesh=mesh, in_specs=in_specs, out_specs=P(("dp", "grp")), check_vma=False
    )
```
